32 devices in a mesh: fibre: 2 (over y), chan: 4 (over z), win: 2 (over x), grp: 2 (over core).
Axes of the slice: x: 2, y: 2, z: 4, core: 2. Of those that a mesh axis runs over, the one named last changes fastest.
Arguments:
- file_rows: bfloat16 [1280, 8192], P(('fibre', 'chan'), 'win'), parts along dimension 0, may hold values from -150 to 150
- channel_list: int32 [1280], P(('fibre', 'chan')), parts along dimension 0, may hold values from 0 to 512, as said below
- filter_taps: bfloat16 [64], replicated, may hold values from -0.75 to 0.75
- source_channels: int32 [8, 64], P(('fibre', 'grp')), parts along dimension 0, may hold values from 0 to 511, as said below
Outputs:
- correlations: float32 [1024, 256, 256], P(('fibre', 'chan', 'win'), 'grp'), parts along dimension 0
The draws below stay inside these ranges and needn't reach their ends.
There are 2 independent parts, one for each index of `fibre`. The reference program is written for one: setup_inputs(seed, part) draws one part's arguments, and reference() takes and returns one part's arrays. A program takes and returns all parts, laid end to end along the dimension named above; an argument that names none is the same for every part. Nothing has to cross between parts.
Inputs may be any that keep to these rules, and one draw needn't show every extreme that they name: `channel_list`: the rows of one device are the 160 consecutive rows d * 160 on; its rows that hold data come first. Every channel appears exactly once over all devices; of one device's rows at most 32 lie in one block of channels b * 128 to (b + 1) * 128 - 1, and some device reaches 32 in every block; every device has rows without data. `source_channels`: all 256 channels are different.
All inputs are finite; a program needn't handle non-finite values.
Results may differ from the reference program's by a relative error of at most 0.0076.
Values may be sent and summed in bfloat16 or wider, within the bound.
A program may use at most 128 MiB of HBM per device.

```python
import math
import jax
import jax.numpy as jnp
from jax import lax

L = 4096
FB = 256
F0 = 8
LAGS = 256
TAPS = 64
HALF = 64
SMOOTH = 8
SRC_GRP = 64
CH_DEV = 128
SLOT = 32
ROWCAP = 160
CHANNELS = 512
GROUPS = 4
SOURCES = 256
WINDOWS = 2
SAMPLES = 8192


def ingest_layout(key):
    chan_count = CHANNELS // CH_DEV
    key_order, key_fill, key_shuffle = jax.random.split(jax.random.fold_in(key, 11), 3)
    order = jax.random.permutation(key_order, chan_count)
    owners = jnp.arange(chan_count, dtype=jnp.int32)
    others = 1 + jnp.mod(3 * owners[:, None] + jnp.arange(3, dtype=jnp.int32)[None, :], chan_count - 1)
    ranks = jnp.concatenate([jnp.zeros((chan_count, 1), jnp.int32), others], axis=1)
    senders = order[ranks]
    owner_keys = jax.random.split(key_fill, chan_count)
    within = jax.vmap(lambda one_key: jax.random.permutation(one_key, CH_DEV))(owner_keys)
    channel = owners[:, None] * CH_DEV + within
    sender_of = jnp.repeat(senders, SLOT, axis=1)
    flat_sender = sender_of.reshape(-1).astype(jnp.int32)
    flat_channel = channel.reshape(-1).astype(jnp.int32)
    ties = jax.random.permutation(key_shuffle, CHANNELS).astype(jnp.int32)
    order_index = jnp.argsort(flat_sender * CHANNELS + ties, stable=True)
    sorted_sender = flat_sender[order_index]
    sorted_channel = flat_channel[order_index]
    counts = jnp.sum((flat_sender[:, None] == owners[None, :]).astype(jnp.int32), axis=0)
    starts = jnp.cumsum(counts) - counts
    position = jnp.arange(CHANNELS, dtype=jnp.int32) - starts[sorted_sender]
    empty = jnp.full((chan_count, ROWCAP), CHANNELS, jnp.int32)
    table = empty.at[sorted_sender, position].set(sorted_channel)
    return table.reshape(-1).astype(jnp.int32)


def draw_channel_list(key, part):
    return ingest_layout(key)


def draw_source_channels(key, part):
    key_pick, key_mix = jax.random.split(jax.random.fold_in(key, 23))
    middle = 1 + jax.random.permutation(key_pick, CHANNELS - 2)[:SOURCES - 2]
    picks = jnp.concatenate([jnp.array([0, CHANNELS - 1], jnp.int32), middle.astype(jnp.int32)])
    return jax.random.permutation(key_mix, picks).reshape(GROUPS, SRC_GRP).astype(jnp.int32)


def draw_file_rows(key, part):
    key_base, key_env = jax.random.split(jax.random.fold_in(key, 31), 2)
    total_rows = ROWCAP * (CHANNELS // CH_DEV)
    values = jnp.clip(jax.random.normal(key_base, (total_rows, SAMPLES), jnp.float32), -5.0, 5.0)
    envelope = jnp.exp(jax.random.uniform(key_env, (total_rows, SAMPLES // 16, 1), jnp.float32, 0.0, math.log(10.0)))
    shaped = values.reshape(total_rows, SAMPLES // 16, 16) * envelope
    return shaped.reshape(total_rows, SAMPLES).astype(jnp.bfloat16)


def centred(rng, dims, width, bound, kind=jnp.bfloat16):
    values = jax.random.normal(rng, dims, jnp.float32) * width
    return jnp.minimum(jnp.maximum(values, -bound), bound).astype(kind)


def setup_inputs(seed: int = 0, part: int = 0) -> dict:
    key_of = jax.random.split(jax.random.key(seed), 5)
    part_splits = jax.random.split(jax.random.fold_in(key_of[4], part), 5)
    return {
        "file_rows": draw_file_rows(jax.random.fold_in(jax.random.fold_in(key_of[4], part), 71), part),
        "channel_list": draw_channel_list(jax.random.fold_in(jax.random.fold_in(key_of[4], part), 71), part),
        "filter_taps": centred(key_of[2], (TAPS,), TAPS ** -0.5, 0.75),
        "source_channels": draw_source_channels(jax.random.fold_in(jax.random.fold_in(key_of[4], part), 71), part),
    }


epsilon = 1e-06
water_level = 0.1

def make_tables():
    samples = jnp.arange(L, dtype=jnp.int32)
    bins = jnp.arange(FB, dtype=jnp.int32) + F0
    phase = jnp.mod(samples[:, None] * bins[None, :], L).astype(jnp.float32) * (2.0 * math.pi / L)
    forward = jnp.concatenate([jnp.cos(phase), -jnp.sin(phase)], axis=1).astype(jnp.bfloat16)
    shifts = jnp.arange(LAGS, dtype=jnp.int32) - LAGS // 2
    turn = jnp.mod(bins[:, None] * shifts[None, :], L).astype(jnp.float32) * (2.0 * math.pi / L)
    inverse = (jnp.concatenate([jnp.cos(turn), -jnp.sin(turn)], axis=0) / math.sqrt(FB)).astype(jnp.bfloat16)
    offsets = jnp.arange(FB, dtype=jnp.int32)
    smoother = (jnp.abs(offsets[:, None] - offsets[None, :]) <= SMOOTH).astype(jnp.float32)
    return (forward, inverse, smoother)

def whiten(window_rows, filter_taps, forward, smoother):
    kernel = filter_taps[::-1].reshape(1, 1, TAPS)
    filtered = lax.conv_general_dilated(window_rows[:, None, :], kernel, (1,), [(TAPS - 1, 0)], dimension_numbers=('NCH', 'OIH', 'NCH'), preferred_element_type=jnp.float32)[:, 0, :]
    magnitude_sum = lax.reduce_window(jnp.abs(filtered), jnp.zeros((), filtered.dtype), lax.add, (1, 2 * HALF + 1), (1, 1), ((0, 0), (HALF, HALF)))
    position = jnp.arange(L, dtype=jnp.int32)
    counts = (jnp.minimum(position, HALF) + jnp.minimum(L - 1 - position, HALF) + 1).astype(jnp.float32)
    normalized = (filtered / (magnitude_sum / counts + epsilon)).astype(jnp.bfloat16)
    spectrum = jnp.dot(normalized, forward, preferred_element_type=jnp.float32)
    real_part = spectrum[:, :FB]
    imag_part = spectrum[:, FB:]
    energy = real_part * real_part + imag_part * imag_part
    smooth = jnp.dot(energy, smoother, precision=lax.Precision.HIGHEST, preferred_element_type=jnp.float32) / lax.optimization_barrier(jnp.sum(smoother, axis=0))
    average = lax.optimization_barrier(jnp.mean(energy, axis=1, keepdims=True))
    factor = lax.rsqrt(smooth + water_level * average + epsilon)
    return (spectrum * jnp.concatenate([factor, factor], axis=1)).astype(jnp.bfloat16)

def correlate(chan_spec, src_spec, inverse):
    chan_real = chan_spec[:, :, :FB].astype(jnp.float32)[:, None]
    chan_imag = chan_spec[:, :, FB:].astype(jnp.float32)[:, None]
    src_real = src_spec[:, :, :FB].astype(jnp.float32)[None]
    src_imag = src_spec[:, :, FB:].astype(jnp.float32)[None]
    product = jnp.concatenate([chan_real * src_real + chan_imag * src_imag, chan_imag * src_real - chan_real * src_imag], axis=-1).astype(jnp.bfloat16)
    channels = chan_spec.shape[0]
    sources = src_spec.shape[0]
    windows = chan_spec.shape[1]
    stacked = product.reshape(channels * sources, windows * 2 * FB)
    result = jnp.dot(stacked, jnp.tile(inverse, (windows, 1)), preferred_element_type=jnp.float32)
    return result.reshape(channels, sources, LAGS)

def reference(file_rows, channel_list, filter_taps, source_channels):
    forward, inverse, smoother = make_tables()
    usable = channel_list < CHANNELS
    target = jnp.where(usable, channel_list, CHANNELS).astype(jnp.int32)
    traces = jnp.zeros((CHANNELS, SAMPLES), jnp.bfloat16).at[target].set(file_rows, mode='drop')
    whitened = whiten(traces.reshape(CHANNELS * WINDOWS, L), filter_taps, forward, smoother)
    whitened = whitened.reshape(CHANNELS, WINDOWS, 2 * FB)
    source_spectra = whitened[source_channels.reshape(-1)]
    blocks = whitened.reshape(CHANNELS // SLOT, SLOT, WINDOWS, 2 * FB)
    result = lax.map(lambda block_rows: correlate(block_rows, source_spectra, inverse), blocks)
    return result.reshape(CHANNELS, SOURCES, LAGS)
```

```python
import functools
import math

import jax
import jax.numpy as jnp
import ml_dtypes
import numpy as np
from jax import lax
from jax.experimental import pallas as pl
from jax.experimental.pallas import tpu as pltpu
from jax.sharding import PartitionSpec as P

L = 4096
FB = 256
F0 = 8
LAGS = 256
TAPS = 64
HALF = 64
SMOOTH = 8
CH_DEV = 128
SEG = 64
CHUNK = 256
TAIL = 16
VMEM_LIMIT = 60 * 1024 * 1024

epsilon = 1e-06
water_level = 0.1


def phase_tables():
    bins = np.arange(FB) + F0
    digits = np.arange(SEG)
    coarse = np.mod(digits[:, None] * SEG * bins[None, :], L) * (2.0 * math.pi / L)
    fine = np.mod(digits[:, None] * bins[None, :], L) * (2.0 * math.pi / L)
    pair = lambda angle: np.concatenate([np.cos(angle), np.sin(angle)], axis=1).astype(np.float32)
    shifts = np.arange(LAGS) - LAGS // 2
    turn = np.mod(bins[:, None] * shifts[None, :], L).astype(np.float32) * np.float32(2.0 * math.pi / L)
    inverse = np.concatenate([np.cos(turn), -np.sin(turn)], axis=0) / math.sqrt(FB)
    return pair(coarse), pair(fine), inverse.astype(ml_dtypes.bfloat16)


def dot(a, b):
    return jnp.dot(a, b, preferred_element_type=jnp.float32)


def iota(shape, axis):
    return lax.broadcasted_iota(jnp.int32, shape, axis)


def whiten_kernel(taps_ref, coarse_ref, fine_ref, labels_ref, rows_ref, out_ref,
                  table, filt, size, normed, toeplitz):
    count = rows_ref.shape[0]

    moved = jnp.broadcast_to(taps_ref[...], (128, 256))
    row = iota((128, 256), 0)
    for bit in range(7):
        moved = jnp.where((row >> bit) & 1 == 1, pltpu.roll(moved, 2**bit, 1), moved)
    moved = moved.astype(jnp.bfloat16)
    here, before = moved[:, :128], moved[:, 128:]
    zero = jnp.zeros((128, 128), jnp.bfloat16)
    toeplitz[0:128, :] = jnp.concatenate([before, zero], axis=1)
    toeplitz[128:256, :] = jnp.concatenate([here, before], axis=1)
    toeplitz[256:384, :] = jnp.concatenate([zero, here], axis=1)

    for start in range(0, L, CHUNK):
        if start == 0:
            part = dot(rows_ref[:, 0:CHUNK], toeplitz[128:384, :])
        else:
            part = dot(rows_ref[:, start - 128 : start + CHUNK], toeplitz[...])
        filt[:, start : start + CHUNK] = part
        size[:, start : start + CHUNK] = jnp.abs(part).astype(jnp.bfloat16)

    def fill(a, carry):
        ca = coarse_ref[pl.ds(a, 1), :FB]
        sa = coarse_ref[pl.ds(a, 1), FB:]
        cb = fine_ref[:, :FB]
        sb = fine_ref[:, FB:]
        where = pl.ds(pl.multiple_of(a * SEG, SEG), SEG)
        table[where, :FB] = (ca * cb - sa * sb).astype(jnp.bfloat16)
        table[where, FB:] = (-(sa * cb + ca * sb)).astype(jnp.bfloat16)
        return carry

    lax.fori_loop(0, L // SEG, fill, 0)

    reach = jnp.abs(iota((512, CHUNK), 0) - 128 - iota((512, CHUNK), 1)) <= HALF
    band = reach.astype(jnp.float32).astype(jnp.bfloat16)
    for start in range(0, L, CHUNK):
        low, high = max(start - 128, 0), min(start + CHUNK + 128, L)
        first = low - (start - 128)
        total = dot(size[:, low:high], band[first : first + high - low])
        position = start + iota((1, CHUNK), 1)
        width = jnp.minimum(position, HALF) + jnp.minimum(L - 1 - position, HALF) + 1
        scale = 1.0 / width.astype(jnp.float32)
        normed[:, start : start + CHUNK] = (
            filt[:, start : start + CHUNK] / (total * scale + epsilon)
        ).astype(jnp.bfloat16)

    spectrum = dot(normed[...], table[...])
    real, imag = spectrum[:, :FB], spectrum[:, FB:]
    energy = real * real + imag * imag
    near = (jnp.abs(iota((FB, FB), 0) - iota((FB, FB), 1)) <= SMOOTH)
    near = near.astype(jnp.float32).astype(jnp.bfloat16)
    upper = energy.astype(jnp.bfloat16)
    left = energy - upper.astype(jnp.float32)
    middle = left.astype(jnp.bfloat16)
    lower = (left - middle.astype(jnp.float32)).astype(jnp.bfloat16)
    total = dot(upper, near) + dot(middle, near) + dot(lower, near)
    k = iota((1, FB), 1)
    width = jnp.minimum(k, SMOOTH) + jnp.minimum(FB - 1 - k, SMOOTH) + 1
    smooth = total / width.astype(jnp.float32)
    level = jnp.sum(energy, axis=1, keepdims=True) * (1.0 / FB)
    factor = lax.rsqrt(smooth + water_level * level + epsilon)
    out_ref[0:count, :FB] = (real * factor).astype(jnp.bfloat16)
    out_ref[0:count, FB:] = (imag * factor).astype(jnp.bfloat16)

    labels = labels_ref[...]
    place = iota((TAIL, 2 * FB), 0)
    digits = jnp.where(place == 0, labels >> 6, jnp.where(place == 1, labels & 63, 0))
    out_ref[count : count + TAIL, :] = digits.astype(jnp.float32).astype(jnp.bfloat16)


def select_kernel(wins, sources_ref, spectra_ref, chan_ref, src_ref):
    blocks = spectra_ref.shape[0]
    count = spectra_ref.shape[1] - TAIL
    channels = chan_ref.shape[0]
    groups, width = sources_ref.shape
    first = lax.axis_index("chan") * CH_DEV + lax.axis_index("win") * channels
    diagonal = iota((width, width), 0) == iota((width, width), 1)
    wanted = [
        jnp.sum(jnp.where(diagonal, sources_ref[g : g + 1, :], 0), axis=1, keepdims=True)
        for g in range(groups)
    ]
    wanted.append(first + iota((channels, 1), 0))
    wanted = jnp.concatenate(wanted, axis=0)
    total = None
    for block in range(blocks):
        digits = spectra_ref[block, count : count + TAIL, :count].astype(jnp.float32)
        labels = (digits[0:1, :] * 64.0 + digits[1:2, :]).astype(jnp.int32)
        pick = (wanted == labels).astype(jnp.float32).astype(jnp.bfloat16)
        part = dot(pick, spectra_ref[block, :count, :])
        total = part if total is None else total + part
    src_ref[...] = total[: groups * width]
    chan_ref[...] = total[groups * width :]


def correlate_kernel(wins, inverse_ref, src_ref, chan_ref, out_ref):
    inverse = inverse_ref[...]
    for c in range(out_ref.shape[0]):
        real = imag = None
        for w in range(wins):
            at = w * 2 * FB
            p, q = src_ref[:, at : at + FB], src_ref[:, at + FB : at + 2 * FB]
            a, b = chan_ref[c : c + 1, at : at + FB], chan_ref[c : c + 1, at + FB : at + 2 * FB]
            re, im = a * p + b * q, b * p - a * q
            real = re if real is None else real + re
            imag = im if imag is None else imag + im
        cross = jnp.concatenate([real.astype(jnp.bfloat16), imag.astype(jnp.bfloat16)], axis=1)
        out_ref[c] = dot(cross, inverse)


def local(file_rows, channel_list, filter_taps, source_channels):
    chan_count = lax.axis_size("chan")
    wins = lax.axis_size("win")
    count = chan_count * (CH_DEV // 4)
    channels = CH_DEV // wins
    groups, width = source_channels.shape
    sources = groups * width
    assert file_rows.shape[1] == L and count <= 2 * FB
    coarse, fine, inverse = phase_tables()

    taps = jnp.pad(filter_taps.astype(jnp.float32), (0, 256 - TAPS)).reshape(1, 256)
    labels = jnp.pad(
        channel_list[:count], (0, 2 * FB - count), constant_values=chan_count * CH_DEV
    ).reshape(1, 2 * FB)

    whole = lambda shape: pl.BlockSpec(shape, lambda i: (0,) * len(shape))
    mine = pl.pallas_call(
        whiten_kernel,
        grid=(1,),
        in_specs=[
            whole((1, 256)),
            whole((SEG, 2 * FB)),
            whole((SEG, 2 * FB)),
            whole((1, 2 * FB)),
            whole((count, L)),
        ],
        out_specs=whole((count + TAIL, 2 * FB)),
        out_shape=jax.ShapeDtypeStruct((count + TAIL, 2 * FB), jnp.bfloat16),
        scratch_shapes=[
            pltpu.VMEM((L, 2 * FB), jnp.bfloat16),
            pltpu.VMEM((count, L), jnp.float32),
            pltpu.VMEM((count, L), jnp.bfloat16),
            pltpu.VMEM((count, L), jnp.bfloat16),
            pltpu.VMEM((384, 256), jnp.bfloat16),
        ],
        compiler_params=pltpu.CompilerParams(vmem_limit_bytes=VMEM_LIMIT),
        name="whiten",
    )(taps, jnp.asarray(coarse), jnp.asarray(fine), labels, file_rows)

    spectra = lax.all_gather(mine, ("chan", "win"), axis=0, tiled=False)
    spectra = spectra.reshape(chan_count, wins, count + TAIL, 2 * FB)

    chan_spec, src_spec = pl.pallas_call(
        functools.partial(select_kernel, wins),
        grid=(wins,),
        in_specs=[
            whole((groups, width)),
            pl.BlockSpec((chan_count, None, count + TAIL, 2 * FB), lambda w: (0, w, 0, 0)),
        ],
        out_specs=[
            pl.BlockSpec((channels, 2 * FB), lambda w: (0, w)),
            pl.BlockSpec((sources, 2 * FB), lambda w: (0, w)),
        ],
        out_shape=[
            jax.ShapeDtypeStruct((channels, wins * 2 * FB), jnp.float32),
            jax.ShapeDtypeStruct((sources, wins * 2 * FB), jnp.float32),
        ],
        compiler_params=pltpu.CompilerParams(vmem_limit_bytes=VMEM_LIMIT),
        name="select",
    )(source_channels, spectra)

    step = 8
    return pl.pallas_call(
        functools.partial(correlate_kernel, wins),
        grid=(channels // step,),
        in_specs=[
            whole((2 * FB, LAGS)),
            whole((sources, wins * 2 * FB)),
            pl.BlockSpec((step, wins * 2 * FB), lambda i: (i, 0)),
        ],
        out_specs=pl.BlockSpec((step, sources, LAGS), lambda i: (i, 0, 0)),
        out_shape=jax.ShapeDtypeStruct((channels, sources, LAGS), jnp.float32),
        compiler_params=pltpu.CompilerParams(vmem_limit_bytes=VMEM_LIMIT),
        name="correlate",
    )(jnp.asarray(inverse), src_spec, chan_spec)


def solution(mesh):
    placed = (P(("fibre", "chan"), "win"), P(("fibre", "chan")), P(), P(("fibre", "grp"), None))
    return jax.shard_map(
        local,
        mesh=mesh,
        in_specs=placed,
        out_specs=P(("fibre", "chan", "win"), "grp", None),
        check_vma=False,
    )
```

```python
import functools
import math

import jax
import jax.numpy as jnp
import ml_dtypes
import numpy as np
from jax import lax
from jax.experimental import pallas as pl
from jax.experimental.pallas import tpu as pltpu
from jax.sharding import PartitionSpec as P

L = 4096
FB = 256
F0 = 8
LAGS = 256
TAPS = 64
HALF = 64
SMOOTH = 8
CH_DEV = 128
SEG = 64
CHUNK = 256
TAIL = 16
VMEM_LIMIT = 60 * 1024 * 1024

epsilon = 1e-06
water_level = 0.1


def phase_tables():
    bins = np.arange(FB) + F0
    digits = np.arange(SEG)
    coarse = np.mod(digits[:, None] * SEG * bins[None, :], L) * (2.0 * math.pi / L)
    fine = np.mod(digits[:, None] * bins[None, :], L) * (2.0 * math.pi / L)
    pair = lambda angle: np.concatenate([np.cos(angle), np.sin(angle)], axis=1).astype(np.float32)
    shifts = np.arange(LAGS) - LAGS // 2
    turn = np.mod(bins[:, None] * shifts[None, :], L).astype(np.float32) * np.float32(2.0 * math.pi / L)
    inverse = np.concatenate([np.cos(turn), -np.sin(turn)], axis=0) / math.sqrt(FB)
    return pair(coarse), pair(fine), inverse.astype(ml_dtypes.bfloat16)


def dot(a, b):
    return jnp.dot(a, b, preferred_element_type=jnp.float32)


def iota(shape, axis):
    return lax.broadcasted_iota(jnp.int32, shape, axis)


def whiten_kernel(taps_ref, coarse_ref, fine_ref, labels_ref, file_ref, out_ref,
                  rows_ref, table, filt, size, normed, toeplitz, wide_taps, wide_labels, sem):
    count = rows_ref.shape[0]
    total_count = count * lax.axis_size("grp")

    begin = pl.multiple_of(lax.axis_index("grp") * count, count)
    fetch = pltpu.make_async_copy(file_ref.at[pl.ds(begin, count), :], rows_ref, sem)
    fetch.start()

    def fill(a, carry):
        ca = coarse_ref[pl.ds(a, 1), :FB]
        sa = coarse_ref[pl.ds(a, 1), FB:]
        cb = fine_ref[:, :FB]
        sb = fine_ref[:, FB:]
        where = pl.ds(pl.multiple_of(a * SEG, SEG), SEG)
        table[where, :FB] = (ca * cb - sa * sb).astype(jnp.bfloat16)
        table[where, FB:] = (-(sa * cb + ca * sb)).astype(jnp.bfloat16)
        return carry

    lax.fori_loop(0, L // SEG, fill, 0)

    wide_taps[...] = jnp.zeros_like(wide_taps)
    wide_taps[:, :TAPS] = taps_ref[...].astype(jnp.float32)
    moved = jnp.broadcast_to(wide_taps[...], (128, 256))
    row = iota((128, 256), 0)
    for bit in range(7):
        moved = jnp.where((row >> bit) & 1 == 1, pltpu.roll(moved, 2**bit, 1), moved)
    moved = moved.astype(jnp.bfloat16)
    here, before = moved[:, :128], moved[:, 128:]
    zero = jnp.zeros((128, 128), jnp.bfloat16)
    toeplitz[0:128, :] = jnp.concatenate([before, zero], axis=1)
    toeplitz[128:256, :] = jnp.concatenate([here, before], axis=1)
    toeplitz[256:384, :] = jnp.concatenate([zero, here], axis=1)

    fetch.wait()
    for start in range(0, L, CHUNK):
        if start == 0:
            part = dot(rows_ref[:, 0:CHUNK], toeplitz[128:384, :])
        else:
            part = dot(rows_ref[:, start - 128 : start + CHUNK], toeplitz[...])
        filt[:, start : start + CHUNK] = part
        size[:, start : start + CHUNK] = jnp.abs(part).astype(jnp.bfloat16)

    reach = jnp.abs(iota((512, CHUNK), 0) - 128 - iota((512, CHUNK), 1)) <= HALF
    band = reach.astype(jnp.float32).astype(jnp.bfloat16)
    for start in range(0, L, CHUNK):
        low, high = max(start - 128, 0), min(start + CHUNK + 128, L)
        first = low - (start - 128)
        total = dot(size[:, low:high], band[first : first + high - low])
        position = start + iota((1, CHUNK), 1)
        width = jnp.minimum(position, HALF) + jnp.minimum(L - 1 - position, HALF) + 1
        scale = 1.0 / width.astype(jnp.float32)
        normed[:, start : start + CHUNK] = (
            filt[:, start : start + CHUNK] / (total * scale + epsilon)
        ).astype(jnp.bfloat16)

    spectrum = dot(normed[...], table[...])
    real, imag = spectrum[:, :FB], spectrum[:, FB:]
    energy = real * real + imag * imag
    near = (jnp.abs(iota((FB, FB), 0) - iota((FB, FB), 1)) <= SMOOTH)
    near = near.astype(jnp.float32).astype(jnp.bfloat16)
    upper = energy.astype(jnp.bfloat16)
    left = energy - upper.astype(jnp.float32)
    middle = left.astype(jnp.bfloat16)
    lower = (left - middle.astype(jnp.float32)).astype(jnp.bfloat16)
    total = dot(upper, near) + dot(middle, near) + dot(lower, near)
    k = iota((1, FB), 1)
    width = jnp.minimum(k, SMOOTH) + jnp.minimum(FB - 1 - k, SMOOTH) + 1
    smooth = total / width.astype(jnp.float32)
    level = jnp.sum(energy, axis=1, keepdims=True) * (1.0 / FB)
    factor = lax.rsqrt(smooth + water_level * level + epsilon)
    out_ref[0:count, :FB] = (real * factor).astype(jnp.bfloat16)
    out_ref[0:count, FB:] = (imag * factor).astype(jnp.bfloat16)

    wide_labels[...] = jnp.zeros_like(wide_labels)
    wide_labels[:, :total_count] = labels_ref[:, :total_count]
    labels = wide_labels[...]
    place = iota((TAIL, 2 * FB), 0)
    digits = jnp.where(place == 0, labels >> 6, jnp.where(place == 1, labels & 63, 0))
    out_ref[count : count + TAIL, :] = digits.astype(jnp.float32).astype(jnp.bfloat16)


def other(index, step):
    for bit in range(step.bit_length()):
        if (step >> bit) & 1:
            index = index + 2**bit - 2 ** (bit + 1) * ((index // 2**bit) % 2)
    return index


def gather_kernel(sizes, mine_ref, out_ref, own_sem, z_sems, x_sems, c_sems):
    zs, xs, cs = sizes
    z, x, c = lax.axis_index("chan"), lax.axis_index("win"), lax.axis_index("grp")

    barrier = pltpu.get_barrier_semaphore()
    for axis, size, index in (("chan", zs, z), ("win", xs, x), ("grp", cs, c)):
        for step in range(1, size):
            pl.semaphore_signal(
                barrier, inc=1, device_id={axis: other(index, step)},
                device_id_type=pl.DeviceIdType.MESH,
            )
    pl.semaphore_wait(barrier, zs + xs + cs - 3)

    def send(source, slot, sems, at, axis, target):
        copy = pltpu.make_async_remote_copy(
            src_ref=source,
            dst_ref=out_ref.at[slot],
            send_sem=sems.at[(0, *at)],
            recv_sem=sems.at[(1, *at)],
            device_id={axis: target},
            device_id_type=pl.DeviceIdType.MESH,
        )
        copy.start()
        return copy

    def pass_on(source, slot, d, copies):
        for e in range(1, xs):
            copies[d, e] = send(source, slot, x_sems, (d, e), "win", other(x, e))

    def share(source, slot, d, e, copies):
        for f in range(1, cs):
            copies[d, e, f] = send(source, slot, c_sems, (d, e, f), "grp", other(c, f))

    own = (z, x, c)
    along_z, along_x, along_c = {}, {}, {}
    pass_on(mine_ref, own, 0, along_x)
    for d in range(1, zs):
        along_z[d] = send(mine_ref, own, z_sems, (d,), "chan", other(z, d))
    share(mine_ref, own, 0, 0, along_c)
    keep = pltpu.make_async_copy(mine_ref, out_ref.at[own], own_sem)
    keep.start()

    def relay_x(d):
        for e in range(1, xs):
            along_x[d, e].wait_recv()
            slot = (other(z, d), other(x, e), c)
            share(out_ref.at[slot], slot, d, e, along_c)

    for d in range(1, zs):
        along_z[d].wait_recv()
        slot = (other(z, d), x, c)
        pass_on(out_ref.at[slot], slot, d, along_x)
        share(out_ref.at[slot], slot, d, 0, along_c)
    for d in range(zs):
        relay_x(d)
    for copy in along_c.values():
        copy.wait_recv()
    for copies in (along_z, along_x, along_c):
        for copy in copies.values():
            copy.wait_send()
    keep.wait()


def select_kernel(wins, sources_ref, spectra_ref, chan_ref, src_ref):
    blocks = spectra_ref.shape[0]
    cores = spectra_ref.shape[1]
    count = spectra_ref.shape[2] - TAIL
    channels = chan_ref.shape[0]
    groups, width = sources_ref.shape
    first = lax.axis_index("chan") * CH_DEV + lax.axis_index("win") * channels
    diagonal = iota((width, width), 0) == iota((width, width), 1)
    wanted = [
        jnp.sum(jnp.where(diagonal, sources_ref[g : g + 1, :], 0), axis=1, keepdims=True)
        for g in range(groups)
    ]
    wanted.append(first + iota((channels, 1), 0))
    wanted = jnp.concatenate(wanted, axis=0)
    total = None
    for block in range(blocks):
        digits = spectra_ref[block, 0, count : count + TAIL, : cores * count].astype(jnp.float32)
        labels = (digits[0:1, :] * 64.0 + digits[1:2, :]).astype(jnp.int32)
        pick = (wanted == labels).astype(jnp.float32).astype(jnp.bfloat16)
        rows = jnp.concatenate([spectra_ref[block, c, :count, :] for c in range(cores)], axis=0)
        part = dot(pick, rows)
        total = part if total is None else total + part
    src_ref[...] = total[: groups * width]
    chan_ref[...] = total[groups * width :]


def correlate_kernel(wins, inverse_ref, src_ref, chan_ref, out_ref):
    inverse = inverse_ref[...]
    for c in range(out_ref.shape[0]):
        real = imag = None
        for w in range(wins):
            at = w * 2 * FB
            p, q = src_ref[:, at : at + FB], src_ref[:, at + FB : at + 2 * FB]
            a, b = chan_ref[c : c + 1, at : at + FB], chan_ref[c : c + 1, at + FB : at + 2 * FB]
            re, im = a * p + b * q, b * p - a * q
            real = re if real is None else real + re
            imag = im if imag is None else imag + im
        cross = jnp.concatenate([real.astype(jnp.bfloat16), imag.astype(jnp.bfloat16)], axis=1)
        out_ref[c] = dot(cross, inverse)


def local(file_rows, channel_list, filter_taps, source_channels):
    chan_count = lax.axis_size("chan")
    wins = lax.axis_size("win")
    count = chan_count * (CH_DEV // 4)
    channels = CH_DEV // wins
    groups, width = source_channels.shape
    sources = groups * width
    assert file_rows.shape[1] == L and count <= 2 * FB
    coarse, fine, inverse = phase_tables()

    cores = lax.axis_size("grp")
    share = count // cores
    whole = lambda shape: pl.BlockSpec(shape, lambda i: (0,) * len(shape))
    mine = pl.pallas_call(
        whiten_kernel,
        grid=(1,),
        in_specs=[
            whole((1, TAPS)),
            whole((SEG, 2 * FB)),
            whole((SEG, 2 * FB)),
            whole((1, channel_list.shape[0])),
            pl.BlockSpec(memory_space=pl.ANY),
        ],
        out_specs=whole((share + TAIL, 2 * FB)),
        out_shape=jax.ShapeDtypeStruct((share + TAIL, 2 * FB), jnp.bfloat16),
        scratch_shapes=[
            pltpu.VMEM((share, L), jnp.bfloat16),
            pltpu.VMEM((L, 2 * FB), jnp.bfloat16),
            pltpu.VMEM((share, L), jnp.float32),
            pltpu.VMEM((share, L), jnp.bfloat16),
            pltpu.VMEM((share, L), jnp.bfloat16),
            pltpu.VMEM((384, 256), jnp.bfloat16),
            pltpu.VMEM((1, 256), jnp.float32),
            pltpu.VMEM((1, 2 * FB), jnp.int32),
            pltpu.SemaphoreType.DMA,
        ],
        compiler_params=pltpu.CompilerParams(vmem_limit_bytes=VMEM_LIMIT),
        name="whiten",
    )(
        filter_taps.reshape(1, TAPS),
        jnp.asarray(coarse),
        jnp.asarray(fine),
        channel_list.reshape(1, -1),
        file_rows,
    )

    block = (share + TAIL, 2 * FB)
    gathered = (chan_count, wins, cores, *block)
    small = math.prod(gathered) * 2 <= 8 * 1024 * 1024
    spectra = pl.pallas_call(
        functools.partial(gather_kernel, (chan_count, wins, cores)),
        in_specs=[pl.BlockSpec(memory_space=pltpu.VMEM)],
        out_specs=pl.BlockSpec(memory_space=pltpu.VMEM if small else pl.ANY),
        out_shape=jax.ShapeDtypeStruct(gathered, jnp.bfloat16),
        scratch_shapes=[
            pltpu.SemaphoreType.DMA,
            pltpu.SemaphoreType.DMA((2, chan_count)),
            pltpu.SemaphoreType.DMA((2, chan_count, wins)),
            pltpu.SemaphoreType.DMA((2, chan_count, wins, cores)),
        ],
        compiler_params=pltpu.CompilerParams(collective_id=0, has_side_effects=True),
        name="gather",
    )(mine)

    chan_spec, src_spec = pl.pallas_call(
        functools.partial(select_kernel, wins),
        grid=(wins,),
        in_specs=[
            whole((groups, width)),
            pl.BlockSpec((chan_count, None, cores, *block), lambda w: (0, w, 0, 0, 0)),
        ],
        out_specs=[
            pl.BlockSpec((channels, 2 * FB), lambda w: (0, w)),
            pl.BlockSpec((sources, 2 * FB), lambda w: (0, w)),
        ],
        out_shape=[
            jax.ShapeDtypeStruct((channels, wins * 2 * FB), jnp.float32),
            jax.ShapeDtypeStruct((sources, wins * 2 * FB), jnp.float32),
        ],
        compiler_params=pltpu.CompilerParams(vmem_limit_bytes=VMEM_LIMIT),
        name="select",
    )(source_channels, spectra)

    step = 8
    return pl.pallas_call(
        functools.partial(correlate_kernel, wins),
        grid=(channels // step,),
        in_specs=[
            whole((2 * FB, LAGS)),
            whole((sources, wins * 2 * FB)),
            pl.BlockSpec((step, wins * 2 * FB), lambda i: (i, 0)),
        ],
        out_specs=pl.BlockSpec((step, sources, LAGS), lambda i: (i, 0, 0)),
        out_shape=jax.ShapeDtypeStruct((channels, sources, LAGS), jnp.float32),
        compiler_params=pltpu.CompilerParams(vmem_limit_bytes=VMEM_LIMIT),
        name="correlate",
    )(jnp.asarray(inverse), src_spec, chan_spec)


def solution(mesh):
    placed = (P(("fibre", "chan"), "win"), P(("fibre", "chan")), P(), P(("fibre", "grp"), None))
    return jax.shard_map(
        local,
        mesh=mesh,
        in_specs=placed,
        out_specs=P(("fibre", "chan", "win"), "grp", None),
        check_vma=False,
    )
```

```python
import functools
import math

import jax
import jax.numpy as jnp
import ml_dtypes
import numpy as np
from jax import lax
from jax.experimental import pallas as pl
from jax.experimental.pallas import tpu as pltpu
from jax.sharding import PartitionSpec as P

L = 4096
FB = 256
F0 = 8
LAGS = 256
TAPS = 64
HALF = 64
SMOOTH = 8
CH_DEV = 128
SEG = 64
FOLD = 4
CHUNK = 256
VMEM_LIMIT = 60 * 1024 * 1024

epsilon = 1e-06
water_level = 0.1


def phase_tables():
    bins = np.arange(FB) + F0
    digits = np.arange(SEG)
    coarse = np.mod(digits[:, None] * SEG * bins[None, :], L) * (2.0 * math.pi / L)
    fine = np.mod(digits[:, None] * bins[None, :], L) * (2.0 * math.pi / L)
    pair = lambda angle: np.concatenate([np.cos(angle), np.sin(angle)], axis=1).astype(np.float32)
    shifts = np.arange(LAGS) - LAGS // 2
    turn = np.mod(bins[:, None] * shifts[None, :], L).astype(np.float32) * np.float32(2.0 * math.pi / L)
    inverse = np.concatenate([np.cos(turn), -np.sin(turn)], axis=0) / math.sqrt(FB)
    return pair(coarse), pair(fine), inverse.astype(ml_dtypes.bfloat16)


def dot(a, b):
    return jnp.dot(a, b, preferred_element_type=jnp.float32)


def iota(shape, axis):
    return lax.broadcasted_iota(jnp.int32, shape, axis)


def whiten_kernel(taps_ref, coarse_ref, fine_ref, labels_ref, file_ref, out_ref, seen_ref,
                  rows_ref, table, filt, size, normed, toeplitz, wide_taps, sem):
    count = rows_ref.shape[0]
    total_count = count * lax.axis_size("grp")

    begin = pl.multiple_of(lax.axis_index("grp") * count, count)
    fetch = pltpu.make_async_copy(file_ref.at[pl.ds(begin, count), :], rows_ref, sem)
    fetch.start()

    def fill(a, carry):
        ca = coarse_ref[pl.ds(a, 1), :FB]
        sa = coarse_ref[pl.ds(a, 1), FB:]
        cb = fine_ref[:, :FB]
        sb = fine_ref[:, FB:]
        where = pl.ds(pl.multiple_of(a * SEG, SEG), SEG)
        table[where, :FB] = (ca * cb - sa * sb).astype(jnp.bfloat16)
        table[where, FB:] = (-(sa * cb + ca * sb)).astype(jnp.bfloat16)
        return carry

    lax.fori_loop(0, L // FOLD // SEG, fill, 0)

    wide_taps[...] = jnp.zeros_like(wide_taps)
    wide_taps[:, :TAPS] = taps_ref[...].astype(jnp.float32)
    moved = jnp.broadcast_to(wide_taps[...], (128, 256))
    row = iota((128, 256), 0)
    for bit in range(7):
        moved = jnp.where((row >> bit) & 1 == 1, pltpu.roll(moved, 2**bit, 1), moved)
    moved = moved.astype(jnp.bfloat16)
    here, before = moved[:, :128], moved[:, 128:]
    zero = jnp.zeros((128, 128), jnp.bfloat16)
    toeplitz[0:128, :] = jnp.concatenate([before, zero], axis=1)
    toeplitz[128:256, :] = jnp.concatenate([here, before], axis=1)
    toeplitz[256:384, :] = jnp.concatenate([zero, here], axis=1)

    fetch.wait()
    for start in range(0, L, CHUNK):
        if start == 0:
            part = dot(rows_ref[:, 0:CHUNK], toeplitz[128:384, :])
        else:
            part = dot(rows_ref[:, start - 128 : start + CHUNK], toeplitz[...])
        filt[:, start : start + CHUNK] = part
        size[:, start : start + CHUNK] = jnp.abs(part).astype(jnp.bfloat16)

    reach = jnp.abs(iota((512, CHUNK), 0) - 128 - iota((512, CHUNK), 1)) <= HALF
    band = reach.astype(jnp.float32).astype(jnp.bfloat16)
    for start in range(0, L, CHUNK):
        low, high = max(start - 128, 0), min(start + CHUNK + 128, L)
        first = low - (start - 128)
        total = dot(size[:, low:high], band[first : first + high - low])
        position = start + iota((1, CHUNK), 1)
        width = jnp.minimum(position, HALF) + jnp.minimum(L - 1 - position, HALF) + 1
        scale = 1.0 / width.astype(jnp.float32)
        fold, at = divmod(start, L // FOLD)
        normed[fold * count : (fold + 1) * count, at : at + CHUNK] = (
            filt[:, start : start + CHUNK] / (total * scale + epsilon)
        ).astype(jnp.bfloat16)

    quarters = dot(normed[...], table[...])
    k = iota((1, FB), 1) + F0
    real = imag = jnp.zeros((count, FB), jnp.float32)
    for fold in range(FOLD):
        turns = (k * fold) % 4
        cosine = jnp.where(turns == 0, 1.0, jnp.where(turns == 2, -1.0, 0.0))
        sine = jnp.where(turns == 1, 1.0, jnp.where(turns == 3, -1.0, 0.0))
        re = quarters[fold * count : (fold + 1) * count, :FB]
        im = quarters[fold * count : (fold + 1) * count, FB:]
        real = real + cosine * re + sine * im
        imag = imag + cosine * im - sine * re
    energy = real * real + imag * imag
    near = (jnp.abs(iota((FB, FB), 0) - iota((FB, FB), 1)) <= SMOOTH)
    near = near.astype(jnp.float32).astype(jnp.bfloat16)
    upper = energy.astype(jnp.bfloat16)
    left = energy - upper.astype(jnp.float32)
    middle = left.astype(jnp.bfloat16)
    lower = (left - middle.astype(jnp.float32)).astype(jnp.bfloat16)
    total = dot(upper, near) + dot(middle, near) + dot(lower, near)
    k = iota((1, FB), 1)
    width = jnp.minimum(k, SMOOTH) + jnp.minimum(FB - 1 - k, SMOOTH) + 1
    smooth = total / width.astype(jnp.float32)
    level = jnp.sum(energy, axis=1, keepdims=True) * (1.0 / FB)
    factor = lax.rsqrt(smooth + water_level * level + epsilon)
    out_ref[0:count, :FB] = (real * factor).astype(jnp.bfloat16)
    out_ref[0:count, FB:] = (imag * factor).astype(jnp.bfloat16)

    seen_ref[...] = jnp.zeros_like(seen_ref)
    seen_ref[:, :total_count] = labels_ref[:, :total_count]


def other(index, step):
    for bit in range(step.bit_length()):
        if (step >> bit) & 1:
            index = index + 2**bit - 2 ** (bit + 1) * ((index // 2**bit) % 2)
    return index


def gather_kernel(sizes, mine_ref, seen_ref, out_ref, labels_ref,
                  own_sems, z_sems, label_sems, x_sems, c_sems):
    zs, xs, cs = sizes
    z, x, c = lax.axis_index("chan"), lax.axis_index("win"), lax.axis_index("grp")

    barrier = pltpu.get_barrier_semaphore()
    for axis, size, index in (("chan", zs, z), ("win", xs, x), ("grp", cs, c)):
        for step in range(1, size):
            pl.semaphore_signal(
                barrier, inc=1, device_id={axis: other(index, step)},
                device_id_type=pl.DeviceIdType.MESH,
            )
    pl.semaphore_wait(barrier, zs + xs + cs - 3)

    def send(source, slot, sems, at, axis, target):
        copy = pltpu.make_async_remote_copy(
            src_ref=source,
            dst_ref=out_ref.at[slot],
            send_sem=sems.at[(0, *at)],
            recv_sem=sems.at[(1, *at)],
            device_id={axis: target},
            device_id_type=pl.DeviceIdType.MESH,
        )
        copy.start()
        return copy

    def pass_on(source, slot, d, copies):
        for e in range(1, xs):
            copies[d, e] = send(source, slot, x_sems, (d, e), "win", other(x, e))

    def share(source, slot, d, e, copies):
        for f in range(1, cs):
            copies[d, e, f] = send(source, slot, c_sems, (d, e, f), "grp", other(c, f))

    own = (z, x, c)
    along_z, along_x, along_c = {}, {}, {}
    pass_on(mine_ref, own, 0, along_x)
    for d in range(1, zs):
        along_z[d] = send(mine_ref, own, z_sems, (d,), "chan", other(z, d))
    share(mine_ref, own, 0, 0, along_c)
    told = []
    for d in range(1, zs):
        copy = pltpu.make_async_remote_copy(
            src_ref=seen_ref,
            dst_ref=labels_ref.at[z],
            send_sem=label_sems.at[0, d],
            recv_sem=label_sems.at[1, d],
            device_id={"chan": other(z, d)},
            device_id_type=pl.DeviceIdType.MESH,
        )
        copy.start()
        told.append(copy)
    keep = pltpu.make_async_copy(mine_ref, out_ref.at[own], own_sems.at[0])
    keep.start()
    keep_labels = pltpu.make_async_copy(seen_ref, labels_ref.at[z], own_sems.at[1])
    keep_labels.start()

    def relay_x(d):
        for e in range(1, xs):
            along_x[d, e].wait_recv()
            slot = (other(z, d), other(x, e), c)
            share(out_ref.at[slot], slot, d, e, along_c)

    for d in range(1, zs):
        along_z[d].wait_recv()
        slot = (other(z, d), x, c)
        pass_on(out_ref.at[slot], slot, d, along_x)
        share(out_ref.at[slot], slot, d, 0, along_c)
    for d in range(zs):
        relay_x(d)
    for copy in along_c.values():
        copy.wait_recv()
    for copies in (along_z, along_x, along_c):
        for copy in copies.values():
            copy.wait_send()
    for copy in told:
        copy.wait()
    keep.wait()
    keep_labels.wait()


def select_kernel(sources_ref, labels_ref, spectra_ref, chan_ref, src_ref):
    blocks = spectra_ref.shape[0]
    cores = spectra_ref.shape[1]
    count = spectra_ref.shape[2]
    channels = chan_ref.shape[0]
    groups, width = sources_ref.shape
    first = lax.axis_index("chan") * CH_DEV + lax.axis_index("win") * channels
    diagonal = iota((width, width), 0) == iota((width, width), 1)
    wanted = [
        jnp.sum(jnp.where(diagonal, sources_ref[g : g + 1, :], 0), axis=1, keepdims=True)
        for g in range(groups)
    ]
    wanted.append(first + iota((channels, 1), 0))
    wanted = jnp.concatenate(wanted, axis=0)
    total = None
    for block in range(blocks):
        pick = (wanted == labels_ref[block, :, : cores * count]).astype(jnp.float32).astype(jnp.bfloat16)
        rows = jnp.concatenate([spectra_ref[block, c] for c in range(cores)], axis=0)
        part = dot(pick, rows)
        total = part if total is None else total + part
    src_ref[...] = total[: groups * width].astype(jnp.bfloat16)
    chan_ref[...] = total[groups * width :]


def correlate_kernel(wins, inverse_ref, src_ref, chan_ref, out_ref):
    inverse = inverse_ref[...]
    for c in range(out_ref.shape[0]):
        real = imag = None
        for w in range(wins):
            at = w * 2 * FB
            p, q = src_ref[:, at : at + FB], src_ref[:, at + FB : at + 2 * FB]
            row = chan_ref[c : c + 1, at : at + 2 * FB].astype(jnp.bfloat16)
            a, b = row[:, :FB], row[:, FB:]
            re, im = a * p + b * q, b * p - a * q
            real = re if real is None else real + re
            imag = im if imag is None else imag + im
        cross = jnp.concatenate([real, imag], axis=1)
        out_ref[c] = dot(cross, inverse)


def local(file_rows, channel_list, filter_taps, source_channels):
    chan_count = lax.axis_size("chan")
    wins = lax.axis_size("win")
    count = chan_count * (CH_DEV // 4)
    channels = CH_DEV // wins
    groups, width = source_channels.shape
    sources = groups * width
    assert file_rows.shape[1] == L and count <= 2 * FB
    coarse, fine, inverse = phase_tables()

    cores = lax.axis_size("grp")
    share = count // cores
    whole = lambda shape: pl.BlockSpec(shape, lambda i: (0,) * len(shape))
    mine, seen = pl.pallas_call(
        whiten_kernel,
        grid=(1,),
        in_specs=[
            whole((1, TAPS)),
            whole((SEG, 2 * FB)),
            whole((SEG, 2 * FB)),
            whole((1, channel_list.shape[0])),
            pl.BlockSpec(memory_space=pl.ANY),
        ],
        out_specs=[whole((share, 2 * FB)), whole((1, 2 * FB))],
        out_shape=[
            jax.ShapeDtypeStruct((share, 2 * FB), jnp.bfloat16),
            jax.ShapeDtypeStruct((1, 2 * FB), jnp.int32),
        ],
        scratch_shapes=[
            pltpu.VMEM((share, L), jnp.bfloat16),
            pltpu.VMEM((L // FOLD, 2 * FB), jnp.bfloat16),
            pltpu.VMEM((share, L), jnp.float32),
            pltpu.VMEM((share, L), jnp.bfloat16),
            pltpu.VMEM((FOLD * share, L // FOLD), jnp.bfloat16),
            pltpu.VMEM((384, 256), jnp.bfloat16),
            pltpu.VMEM((1, 256), jnp.float32),
            pltpu.SemaphoreType.DMA,
        ],
        compiler_params=pltpu.CompilerParams(vmem_limit_bytes=VMEM_LIMIT),
        name="whiten",
    )(
        filter_taps.reshape(1, TAPS),
        jnp.asarray(coarse),
        jnp.asarray(fine),
        channel_list.reshape(1, -1),
        file_rows,
    )

    block = (share, 2 * FB)
    gathered = (chan_count, wins, cores, *block)
    small = math.prod(gathered) * 2 <= 8 * 1024 * 1024
    spectra, labels = pl.pallas_call(
        functools.partial(gather_kernel, (chan_count, wins, cores)),
        in_specs=[pl.BlockSpec(memory_space=pltpu.VMEM)] * 2,
        out_specs=[
            pl.BlockSpec(memory_space=pltpu.VMEM if small else pl.ANY),
            pl.BlockSpec(memory_space=pltpu.VMEM),
        ],
        out_shape=[
            jax.ShapeDtypeStruct(gathered, jnp.bfloat16),
            jax.ShapeDtypeStruct((chan_count, 1, 2 * FB), jnp.int32),
        ],
        scratch_shapes=[
            pltpu.SemaphoreType.DMA((2,)),
            pltpu.SemaphoreType.DMA((2, chan_count)),
            pltpu.SemaphoreType.DMA((2, chan_count)),
            pltpu.SemaphoreType.DMA((2, chan_count, wins)),
            pltpu.SemaphoreType.DMA((2, chan_count, wins, cores)),
        ],
        compiler_params=pltpu.CompilerParams(collective_id=0, has_side_effects=True),
        name="gather",
    )(mine, seen)

    chan_spec, src_spec = pl.pallas_call(
        select_kernel,
        grid=(wins,),
        in_specs=[
            whole((groups, width)),
            whole((chan_count, 1, 2 * FB)),
            pl.BlockSpec((chan_count, None, cores, *block), lambda w: (0, w, 0, 0, 0)),
        ],
        out_specs=[
            pl.BlockSpec((channels, 2 * FB), lambda w: (0, w)),
            pl.BlockSpec((sources, 2 * FB), lambda w: (0, w)),
        ],
        out_shape=[
            jax.ShapeDtypeStruct((channels, wins * 2 * FB), jnp.float32),
            jax.ShapeDtypeStruct((sources, wins * 2 * FB), jnp.bfloat16),
        ],
        compiler_params=pltpu.CompilerParams(vmem_limit_bytes=VMEM_LIMIT),
        name="select",
    )(source_channels, labels, spectra)

    step = 8
    return pl.pallas_call(
        functools.partial(correlate_kernel, wins),
        grid=(channels // step,),
        in_specs=[
            whole((2 * FB, LAGS)),
            whole((sources, wins * 2 * FB)),
            pl.BlockSpec((step, wins * 2 * FB), lambda i: (i, 0)),
        ],
        out_specs=pl.BlockSpec((step, sources, LAGS), lambda i: (i, 0, 0)),
        out_shape=jax.ShapeDtypeStruct((channels, sources, LAGS), jnp.float32),
        compiler_params=pltpu.CompilerParams(vmem_limit_bytes=VMEM_LIMIT),
        name="correlate",
    )(jnp.asarray(inverse), src_spec, chan_spec)


def solution(mesh):
    placed = (P(("fibre", "chan"), "win"), P(("fibre", "chan")), P(), P(("fibre", "grp"), None))
    return jax.shard_map(
        local,
        mesh=mesh,
        in_specs=placed,
        out_specs=P(("fibre", "chan", "win"), "grp", None),
        check_vma=False,
    )
```
